32 devices in a mesh: strip: 8 (over y, x, core), mode: 4 (over z).
Axes of the slice: x: 2, y: 2, z: 4, core: 2. Of those that a mesh axis runs over, the one named last changes fastest.
Arguments:
- object_field: float32 [2, 2048, 384], P(None, 'strip'), may hold values from -5 to 5
- probe_modes: float32 [2, 8, 256, 256], P(None, 'mode'), may hold values from -2.5 to 2.5
- measured: float32 [8, 4, 256, 256], P('strip'), may hold values from 0.1 to 27
- positions: int32 [8, 4, 2], P('strip'), may hold values from 0 to 128, as said below
Outputs:
- object_new: float32 [2, 2048, 384], P(None, 'strip')
The draws below stay inside these ranges and needn't reach their ends.
Inputs may be any that keep to these rules, and one draw needn't show every extreme that they name: positions[s,k,0] is the first row of window k within strip s and positions[s,k,1] its first column; the windows of every strip form a two by two raster with small offsets: windows 0 and 3 start at row 128, windows 1 and 2 at row 0, window 1 at column 128, window 3 at most 16 columns left of it, windows 0 and 2 at columns 0 to 16.
All inputs are finite; a program needn't handle non-finite values.
Results may differ from the reference program's by a relative error of at most 0.0001.
Values sent between devices are 32-bit elements; how exact they have to be, the bound alone decides.
A program may use at most 128 MiB of HBM per device.

```python
import jax
import jax.numpy as jnp
from jax import lax

WINDOW_SIDE = 256
MODES = 8
SR = 256
W = 384
HALO = 128
POS = 4
ITERS = 3
STRIPS = 8
ROWS = 2048


def draw_positions(key, part):
    jitter_key = jax.random.fold_in(key, 7)
    row_most = SR + HALO - WINDOW_SIDE
    col_most = W - WINDOW_SIDE
    jitter = max(WINDOW_SIDE // 16, 1)
    offsets = jax.random.randint(jitter_key, (STRIPS, 3), 0, jitter + 1, dtype=jnp.int32)
    zeros_col = jnp.zeros((STRIPS,), jnp.int32)
    rows_drawn = jnp.stack([zeros_col + row_most, zeros_col, zeros_col, zeros_col + row_most], axis=1)
    cols_drawn = jnp.stack([offsets[:, 0], zeros_col + col_most, offsets[:, 1], col_most - offsets[:, 2]], axis=1)
    cols_drawn = jnp.clip(cols_drawn, 0, col_most)
    return jnp.stack([rows_drawn, cols_drawn], axis=-1).astype(jnp.int32)


def draw_measured(key, part):
    base_key, window_key = jax.random.split(jax.random.fold_in(key, 11))
    shape_full = (STRIPS, POS, WINDOW_SIDE, WINDOW_SIDE)
    base_values = jnp.exp(jax.random.uniform(base_key, shape_full, jnp.float32, jnp.log(0.1), jnp.log(3.0)))
    spread = jnp.exp(jax.random.uniform(window_key, (STRIPS, POS, 1, 1), jnp.float32, 0.0, jnp.log(3.0)))
    strip_ramp = 1.0 + 2.0 * jnp.arange(STRIPS, dtype=jnp.float32) / max(STRIPS - 1, 1)
    return base_values * spread * strip_ramp[:, None, None, None]


def levels(rng, extent, shards, low, high):
    gain, own = 1.0, jax.random.fold_in(rng, 6)
    for dim, shards_of in shards:
        draws = jnp.exp(jax.random.uniform(jax.random.fold_in(own, dim), (shards_of,), jnp.float32, low / len(shards), high / len(shards)))
        gain = gain * jnp.repeat(draws, extent[dim] // shards_of).reshape([-1 if axis == dim else 1 for axis in range(len(extent))])
    return gain


def normal_values(key, shape, scale, bound, shards=(), kind=jnp.bfloat16):
    array = jax.random.normal(key, shape, jnp.float32) * scale
    if len(shards) > 0:
        array = levels(key, shape, shards, -0.22, 0.18) * array
    return jnp.clip(array, min=-bound, max=bound).astype(kind)


def setup_inputs(seed: int = 0) -> dict:
    splits = jax.random.split(jax.random.key(seed), 5)
    object_field = normal_values(splits[0], (2, ROWS, W), 0.7, 5.0, ((1, 8),), jnp.float32)
    probe_modes = normal_values(splits[1], (2, MODES, WINDOW_SIDE, WINDOW_SIDE), 0.18, 2.5, ((1, 4),), jnp.float32)
    measured = draw_measured(jax.random.fold_in(splits[4], 71), 0)
    positions = draw_positions(jax.random.fold_in(splits[4], 71), 0)
    return dict(object_field=object_field, probe_modes=probe_modes, measured=measured, positions=positions)


regularizer = 0.1
step_scale = 0.3
epsilon = 1e-06

def gradient_window(padded_object, complex_probe, measured_window, row_begin, column_begin):
    patch = lax.dynamic_slice(padded_object, (row_begin, column_begin), (WINDOW_SIDE, WINDOW_SIDE))
    exit_wave = complex_probe * patch[None]
    far_field = jnp.fft.fft2(exit_wave, norm='ortho')
    probe_power = lax.optimization_barrier(jnp.sum(far_field.real ** 2 + far_field.imag ** 2, axis=0))
    object_update = jnp.sqrt((measured_window + regularizer) / (probe_power + regularizer)) - 1.0
    delta = jnp.fft.ifft2(object_update[None] * far_field, norm='ortho')
    return lax.optimization_barrier(jnp.sum(jnp.conj(complex_probe) * delta, axis=0))

def reference(object_field, probe_modes, measured, positions):
    complex_probe = probe_modes[0] + 1j * probe_modes[1]
    offsets = SR * jnp.arange(STRIPS, dtype=jnp.int32)
    every_row_start = (positions[:, :, 0] + offsets[:, None]).reshape(-1).astype(jnp.int32)
    every_column_start = positions[:, :, 1].reshape(-1).astype(jnp.int32)
    measured_patterns = measured.reshape(-1, WINDOW_SIDE, WINDOW_SIDE)
    field = object_field
    for iteration in range(ITERS):
        padded_object = jnp.pad(field[0] + 1j * field[1], ((0, HALO), (0, 0)))

        def single_window(element):
            return gradient_window(padded_object, complex_probe, element[0], element[1], element[2])
        window_gradients = lax.map(single_window, (measured_patterns, every_row_start, every_column_start))

        def accumulate(counter, total):
            start = (every_row_start[counter], every_column_start[counter])
            current = lax.dynamic_slice(total, start, (WINDOW_SIDE, WINDOW_SIDE))
            return lax.dynamic_update_slice(total, current + window_gradients[counter], start)
        total = lax.fori_loop(0, every_row_start.shape[0], accumulate, jnp.zeros_like(padded_object))
        gradient = total[:ROWS]
        stacked = jnp.stack([gradient.real, gradient.imag])
        square_sum = jnp.sum(stacked * stacked)
        factor = step_scale / jnp.sqrt(square_sum / (ROWS * W) + epsilon)
        field = field + factor * stacked
    return field
```

```python
import functools

import jax
import jax.numpy as jnp
import numpy as np
from jax import lax
from jax.experimental import pallas as pl
from jax.experimental.pallas import tpu as pltpu
from jax.sharding import PartitionSpec as P

HALO = 128
ITERS = 3

regularizer = 0.1
step_scale = 0.3
epsilon = 1e-06
f32 = jnp.float32
bf16 = jnp.bfloat16


def tables(n):
    half = n // 2
    k = np.arange(half)
    angle = 2.0 * np.pi * (np.outer(k, k) % half) / half
    c = np.cos(angle) / np.sqrt(n)
    s = np.sin(angle) / np.sqrt(n)
    right_f = np.block([[c, -s], [s, c]])
    right_i = np.block([[c, s], [-s, c]])
    turn = 2.0 * np.pi * k / n
    wr, wi = np.cos(turn), -np.sin(turn)

    def split(t):
        t = jnp.asarray(t, f32)
        high = t.astype(bf16)
        low = (t - high.astype(f32)).astype(bf16)
        return high, low

    rf, ri = split(right_f), split(right_i)
    lf, li = split(right_f.T), split(right_i.T)
    rights = jnp.stack([rf[0], rf[1], ri[0], ri[1]])
    lefts = jnp.stack([jnp.concatenate(lf), jnp.concatenate(li)])
    lanes = jnp.asarray(np.stack([wr, wi]), f32)[:, None, :]
    subs = jnp.asarray(np.broadcast_to(np.stack([wr, wi])[:, :, None], (2, half, n)), f32)
    return rights, lefts, lanes, subs


def split2(x):
    high = x.astype(bf16)
    low = (x - high.astype(f32)).astype(bf16)
    return high, low


def dot(a, b):
    return jnp.dot(a, b, preferred_element_type=f32)


def right_dot(x, t_high, t_low):
    high, low = split2(x)
    return dot(high, t_high) + (dot(low, t_high) + dot(high, t_low))


def left_dot(t_both, x):
    n = x.shape[0]
    high, low = split2(x)
    both = dot(t_both, high)
    return both[:n] + (both[n:] + dot(t_both[:n], low))


def gradient_kernel(col_ref, obj_ref, probe_ref, meas_ref, rights, lefts, lanes, subs, out_ref, far_ref, power_ref, acc_ref, patch_ref):
    n = meas_ref.shape[0]
    half = n // 2
    width = obj_ref.shape[2]
    modes = probe_ref.shape[1]
    col = col_ref[0]
    back = jnp.where(col == 0, 0, width - col)
    for part in range(2):
        patch_ref[part] = pltpu.roll(obj_ref[part], back, 1)[:, :n]
    power_ref[...] = jnp.zeros_like(power_ref)
    acc_ref[...] = jnp.zeros_like(acc_ref)
    cat = jnp.concatenate

    def forward(m):
        pr, pi = probe_ref[0, m], probe_ref[1, m]
        xr, xi = patch_ref[0], patch_ref[1]
        er = pr * xr - pi * xi
        ei = pr * xi + pi * xr
        wr, wi = lanes[0], lanes[1]
        ar, ai = er[:, :half] + er[:, half:], ei[:, :half] + ei[:, half:]
        br, bi = er[:, :half] - er[:, half:], ei[:, :half] - ei[:, half:]
        even = right_dot(cat([ar, ai], 1), rights[0], rights[1])
        odd = right_dot(cat([br * wr - bi * wi, br * wi + bi * wr], 1), rights[0], rights[1])
        yr = cat([even[:, :half], odd[:, :half]], 1)
        yi = cat([even[:, half:], odd[:, half:]], 1)
        wr, wi = subs[0], subs[1]
        ar, ai = yr[:half] + yr[half:], yi[:half] + yi[half:]
        br, bi = yr[:half] - yr[half:], yi[:half] - yi[half:]
        even = left_dot(lefts[0], cat([ar, ai], 0))
        odd = left_dot(lefts[0], cat([br * wr - bi * wi, br * wi + bi * wr], 0))
        far_ref[m, 0] = even
        far_ref[m, 1] = odd
        return cat(
            [
                even[:half] * even[:half] + even[half:] * even[half:],
                odd[:half] * odd[:half] + odd[half:] * odd[half:],
            ],
            0,
        )

    def forward_two(i, carry):
        power_ref[...] += forward(2 * i) + forward(2 * i + 1)
        return carry

    lax.fori_loop(0, modes // 2, forward_two, 0)
    power_ref[...] = jnp.sqrt((meas_ref[...] + regularizer) / (power_ref[...] + regularizer)) - 1.0

    def backward(m):
        ce, co = power_ref[:half], power_ref[half:]
        ce, co = cat([ce, ce], 0), cat([co, co], 0)
        even = left_dot(lefts[1], ce * far_ref[m, 0])
        odd = left_dot(lefts[1], co * far_ref[m, 1])
        wr, wi = subs[0], subs[1]
        ar, ai = even[:half], even[half:]
        br, bi = odd[:half], odd[half:]
        tr, ti = br * wr + bi * wi, bi * wr - br * wi
        yr = cat([ar + tr, ar - tr], 0)
        yi = cat([ai + ti, ai - ti], 0)
        even = right_dot(cat([yr[:, :half], yi[:, :half]], 1), rights[2], rights[3])
        odd = right_dot(cat([yr[:, half:], yi[:, half:]], 1), rights[2], rights[3])
        wr, wi = lanes[0], lanes[1]
        ar, ai = even[:, :half], even[:, half:]
        br, bi = odd[:, :half], odd[:, half:]
        tr, ti = br * wr + bi * wi, bi * wr - br * wi
        dr = cat([ar + tr, ar - tr], 1)
        di = cat([ai + ti, ai - ti], 1)
        pr, pi = probe_ref[0, m], probe_ref[1, m]
        return pr * dr + pi * di, pr * di - pi * dr

    def backward_two(i, carry):
        gr, gi = backward(2 * i)
        hr, hi = backward(2 * i + 1)
        acc_ref[0] += gr + hr
        acc_ref[1] += gi + hi
        return carry

    lax.fori_loop(0, modes // 2, backward_two, 0)
    for part in range(2):
        wide = cat([acc_ref[part], jnp.zeros((n, width - n), f32)], 1)
        out_ref[part] = pltpu.roll(wide, col, 1)


def window_gradient(col, rows, probe, meas, consts):
    n = meas.shape[0]
    modes = probe.shape[1]
    vmem = pl.BlockSpec(memory_space=pltpu.VMEM)
    flops = modes * 2 * 4 * 3 * 2 * n**3
    return pl.pallas_call(
        gradient_kernel,
        out_shape=jax.ShapeDtypeStruct(rows.shape, f32),
        in_specs=[pl.BlockSpec(memory_space=pltpu.SMEM)] + [vmem] * 7,
        out_specs=vmem,
        scratch_shapes=[
            pltpu.VMEM((modes, 2, n, n), f32),
            pltpu.VMEM((n, n), f32),
            pltpu.VMEM((2, n, n), f32),
            pltpu.VMEM((2, n, n), f32),
        ],
        cost_estimate=pl.CostEstimate(flops=flops, bytes_accessed=8 * modes * n * n, transcendentals=n * n),
        compiler_params=pltpu.CompilerParams(vmem_limit_bytes=48 * 2**20),
        name="window_gradient",
    )(col, rows, probe, meas, *consts)


def body(object_field, probe_modes, measured, positions):
    strips, group = lax.axis_size("strip"), lax.axis_size("mode")
    stripe_rows, width = object_field.shape[1:]
    n = probe_modes.shape[2]
    local = probe_modes.shape[1]
    slots = positions.shape[1]
    copies = group // slots
    halo = HALO
    s, m = lax.axis_index("strip"), lax.axis_index("mode")
    side = s % 2
    q = m // copies
    mine = (q // 2) == side
    consts = tables(n)
    partner = [(i, i ^ 1) for i in range(strips)]

    def window_of(which):
        upper = jnp.where(which == 0, 2, 1)
        lower = jnp.where(which == 0, 0, 3)
        return jnp.where(q % 2 == 0, upper, lower)

    share = n // strips
    piece = lax.dynamic_slice_in_dim(probe_modes, s * share, share, axis=2)
    pieces = lax.all_gather(piece, ("strip", "mode"))
    pieces = pieces.reshape(strips, group, 2, local, share, n)
    probe = pieces.transpose(2, 1, 3, 0, 4, 5).reshape(2, group * local, n, n)

    below = lax.ppermute(object_field[:, :halo], "strip", [(i + 1, i) for i in range(strips - 1)])
    frame = jnp.concatenate([object_field, below], axis=1)
    own_rows = jnp.where(q % 2 == 0, frame[:, :stripe_rows], frame[:, halo:])
    theirs = lax.ppermute(own_rows, "strip", partner)
    rows = jnp.where(mine, own_rows, theirs)

    pick = lambda which: lax.dynamic_index_in_dim(measured[0], window_of(which), 0, keepdims=False)
    meas = jnp.where(mine, pick(side), lax.ppermute(pick(1 - side), "strip", partner))
    meas = meas.reshape(n // 2, 2, n // 2, 2).transpose(1, 0, 3, 2).reshape(n, n)
    at = lambda which: lax.dynamic_index_in_dim(positions[0, :, 1], window_of(which), 0)
    col = jnp.where(mine, at(side), lax.ppermute(at(1 - side), "strip", partner))

    forth = []
    for i in range(strips):
        for j in range(group):
            if j + copies < group:
                forth.append((i * group + j, i * group + j + copies))
            elif i + 2 < strips:
                forth.append((i * group + j, (i + 2) * group + j + copies - group))
    back = [(b, a) for a, b in forth]
    last = jnp.logical_and(s >= strips - 2, q == slots - 1)
    both = ("strip", "mode")
    cells = stripe_rows * strips * width
    for iteration in range(ITERS):
        mine_grad = window_gradient(col, rows, probe, meas, consts)
        pair = mine_grad + lax.ppermute(mine_grad, "strip", partner)
        from_prev = lax.ppermute(pair[:, halo:], both, forth)
        from_next = lax.ppermute(pair[:, :halo], both, back)
        top = pair[:, :halo] + from_prev
        bottom = jnp.where(last, 0.0, pair[:, halo:] + from_next)
        square_sum = lax.psum(jnp.sum(top * top), both) / (2 * copies)
        factor = step_scale / jnp.sqrt(square_sum / cells + epsilon)
        rows = rows + factor * jnp.concatenate([top, bottom], axis=1)

    part_rows = halo // 2
    mine_part = lax.dynamic_slice_in_dim(rows, side * part_rows, part_rows, axis=1)
    parts = lax.all_gather(mine_part, "mode")[::copies]
    keep = lax.dynamic_slice_in_dim(parts, 2 * side, 2, axis=0)
    give = lax.dynamic_slice_in_dim(parts, 2 * (1 - side), 2, axis=0)
    got = lax.ppermute(give, "strip", partner)
    low = jnp.where(side == 0, keep, got)
    high = jnp.where(side == 0, got, keep)
    whole = jnp.concatenate([low, high], axis=2)
    return whole.transpose(1, 0, 2, 3).reshape(2, stripe_rows, width)


def solution(mesh):
    return jax.shard_map(
        body,
        mesh=mesh,
        in_specs=(
            P(None, "strip", None),
            P(None, "mode", None, None),
            P("strip", None, None, None),
            P("strip", None, None),
        ),
        out_specs=P(None, "strip", None),
        check_vma=False,
    )
```

```python
import functools

import jax
import jax.numpy as jnp
import numpy as np
from jax import lax
from jax.experimental import pallas as pl
from jax.experimental.pallas import tpu as pltpu
from jax.sharding import PartitionSpec as P

HALO = 128
ITERS = 3

regularizer = 0.1
step_scale = 0.3
epsilon = 1e-06
f32 = jnp.float32
bf16 = jnp.bfloat16
MESH = pl.DeviceIdType.MESH


def tables(n):
    half = n // 2
    k = np.arange(half)
    angle = 2.0 * np.pi * (np.outer(k, k) % half) / half
    c = np.cos(angle) / np.sqrt(n)
    s = np.sin(angle) / np.sqrt(n)
    right_f = np.block([[c, -s], [s, c]])
    right_i = np.block([[c, s], [-s, c]])
    turn = 2.0 * np.pi * k / n
    wr, wi = np.cos(turn), -np.sin(turn)

    def split(t):
        t = jnp.asarray(t, f32)
        high = t.astype(bf16)
        low = (t - high.astype(f32)).astype(bf16)
        return high, low

    rf, ri = split(right_f), split(right_i)
    lf, li = split(right_f.T), split(right_i.T)
    rights = jnp.stack([rf[0], rf[1], ri[0], ri[1]])
    lefts = jnp.stack([jnp.concatenate(lf), jnp.concatenate(li)])
    lanes = jnp.asarray(np.stack([wr, wi]), f32)[:, None, :]
    subs = jnp.asarray(np.broadcast_to(np.stack([wr, wi])[:, :, None], (2, half, n)), f32)
    return rights, lefts, lanes, subs


def split2(x):
    high = x.astype(bf16)
    low = (x - high.astype(f32)).astype(bf16)
    return high, low


def dot(a, b):
    return jnp.dot(a, b, preferred_element_type=f32)


def right_dot(x, t_high, t_low):
    high, low = split2(x)
    return dot(high, t_high) + (dot(low, t_high) + dot(high, t_low))


def left_dot(t_both, x):
    n = x.shape[0]
    high, low = split2(x)
    both = dot(t_both, high)
    return both[:n] + (both[n:] + dot(t_both[:n], low))


def gradient_kernel(col_ref, obj_ref, probe_ref, meas_ref, rights, lefts, lanes, subs, out_ref, far_ref, power_ref, acc_ref, patch_ref):
    n = meas_ref.shape[0]
    half = n // 2
    width = obj_ref.shape[2]
    modes = probe_ref.shape[1]
    col = col_ref[0]
    back = jnp.where(col == 0, 0, width - col)
    for part in range(2):
        patch_ref[part] = pltpu.roll(obj_ref[part], back, 1)[:, :n]
    power_ref[...] = jnp.zeros_like(power_ref)
    acc_ref[...] = jnp.zeros_like(acc_ref)
    cat = jnp.concatenate

    def forward(m):
        pr, pi = probe_ref[0, m], probe_ref[1, m]
        xr, xi = patch_ref[0], patch_ref[1]
        er = pr * xr - pi * xi
        ei = pr * xi + pi * xr
        wr, wi = lanes[0], lanes[1]
        ar, ai = er[:, :half] + er[:, half:], ei[:, :half] + ei[:, half:]
        br, bi = er[:, :half] - er[:, half:], ei[:, :half] - ei[:, half:]
        even = right_dot(cat([ar, ai], 1), rights[0], rights[1])
        odd = right_dot(cat([br * wr - bi * wi, br * wi + bi * wr], 1), rights[0], rights[1])
        yr = cat([even[:, :half], odd[:, :half]], 1)
        yi = cat([even[:, half:], odd[:, half:]], 1)
        wr, wi = subs[0], subs[1]
        ar, ai = yr[:half] + yr[half:], yi[:half] + yi[half:]
        br, bi = yr[:half] - yr[half:], yi[:half] - yi[half:]
        even = left_dot(lefts[0], cat([ar, ai], 0))
        odd = left_dot(lefts[0], cat([br * wr - bi * wi, br * wi + bi * wr], 0))
        far_ref[m, 0] = even
        far_ref[m, 1] = odd
        return cat(
            [
                even[:half] * even[:half] + even[half:] * even[half:],
                odd[:half] * odd[:half] + odd[half:] * odd[half:],
            ],
            0,
        )

    def forward_two(i, carry):
        power_ref[...] += forward(2 * i) + forward(2 * i + 1)
        return carry

    lax.fori_loop(0, modes // 2, forward_two, 0)
    power_ref[...] = jnp.sqrt((meas_ref[...] + regularizer) / (power_ref[...] + regularizer)) - 1.0

    def backward(m):
        ce, co = power_ref[:half], power_ref[half:]
        ce, co = cat([ce, ce], 0), cat([co, co], 0)
        even = left_dot(lefts[1], ce * far_ref[m, 0])
        odd = left_dot(lefts[1], co * far_ref[m, 1])
        wr, wi = subs[0], subs[1]
        ar, ai = even[:half], even[half:]
        br, bi = odd[:half], odd[half:]
        tr, ti = br * wr + bi * wi, bi * wr - br * wi
        yr = cat([ar + tr, ar - tr], 0)
        yi = cat([ai + ti, ai - ti], 0)
        even = right_dot(cat([yr[:, :half], yi[:, :half]], 1), rights[2], rights[3])
        odd = right_dot(cat([yr[:, half:], yi[:, half:]], 1), rights[2], rights[3])
        wr, wi = lanes[0], lanes[1]
        ar, ai = even[:, :half], even[:, half:]
        br, bi = odd[:, :half], odd[:, half:]
        tr, ti = br * wr + bi * wi, bi * wr - br * wi
        dr = cat([ar + tr, ar - tr], 1)
        di = cat([ai + ti, ai - ti], 1)
        pr, pi = probe_ref[0, m], probe_ref[1, m]
        return pr * dr + pi * di, pr * di - pi * dr

    def backward_two(i, carry):
        gr, gi = backward(2 * i)
        hr, hi = backward(2 * i + 1)
        acc_ref[0] += gr + hr
        acc_ref[1] += gi + hi
        return carry

    lax.fori_loop(0, modes // 2, backward_two, 0)
    for part in range(2):
        wide = cat([acc_ref[part], jnp.zeros((n, width - n), f32)], 1)
        out_ref[part] = pltpu.roll(wide, col, 1)


def window_gradient(col, rows, probe, meas, consts):
    n = meas.shape[0]
    modes = probe.shape[1]
    vmem = pl.BlockSpec(memory_space=pltpu.VMEM)
    flops = modes * 2 * 4 * 3 * 2 * n**3
    return pl.pallas_call(
        gradient_kernel,
        out_shape=jax.ShapeDtypeStruct(rows.shape, f32),
        in_specs=[pl.BlockSpec(memory_space=pltpu.SMEM)] + [vmem] * 7,
        out_specs=vmem,
        scratch_shapes=[
            pltpu.VMEM((modes, 2, n, n), f32),
            pltpu.VMEM((n, n), f32),
            pltpu.VMEM((2, n, n), f32),
            pltpu.VMEM((2, n, n), f32),
        ],
        cost_estimate=pl.CostEstimate(flops=flops, bytes_accessed=8 * modes * n * n, transcendentals=n * n),
        compiler_params=pltpu.CompilerParams(vmem_limit_bytes=48 * 2**20),
        name="window_gradient",
    )(col, rows, probe, meas, *consts)


def exchange_kernel(copies, slots, cells, g_ref, rows_ref, out_ref, pair, from_partner, from_prev, from_next, own, other, tile, tiles_a, sum_a, tiles_b, partner_sems, chain_sems, back_sems, a_send, a_recv, b_send, b_recv):
    strips, group = lax.axis_size("strip"), lax.axis_size("mode")
    s, m = lax.axis_index("strip"), lax.axis_index("mode")
    h, q = s % 2, m // copies
    width = g_ref.shape[-1]
    partner = (s + 1 - 2 * h, m)
    inner_next, inner_prev = q < slots - 1, q > 0
    has_next = jnp.logical_or(inner_next, s < strips - 2)
    has_prev = jnp.logical_or(inner_prev, s >= 2)
    cross = (slots - 1) * copies
    after = (jnp.where(inner_next, s, s + 2), jnp.where(inner_next, m + copies, m - cross))
    before = (jnp.where(inner_prev, s, s - 2), jnp.where(inner_prev, m - copies, m + cross))
    cross_next = jnp.logical_and(has_next, jnp.logical_not(inner_next))
    cross_prev = jnp.logical_and(has_prev, jnp.logical_not(inner_prev))

    barrier = pltpu.get_barrier_semaphore()

    def greet(device):
        pl.semaphore_signal(barrier, inc=1, device_id=device, device_id_type=MESH)

    for d in range(1, group):
        greet((s, (m + d) % group))
    for d in range(1, strips):
        greet(((s + d) % strips, m))

    @pl.when(cross_next)
    def _():
        greet(after)

    @pl.when(cross_prev)
    def _():
        greet(before)

    extra = jnp.where(cross_next, 1, 0) + jnp.where(cross_prev, 1, 0)
    pl.semaphore_wait(barrier, group + strips - 2 + extra)

    def send(src, dst, send_sem, recv_sem, device):
        return pltpu.make_async_remote_copy(
            src_ref=src, dst_ref=dst, send_sem=send_sem, recv_sem=recv_sem,
            device_id=device, device_id_type=MESH,
        )

    first = send(g_ref.at[:, :, 1 - h], from_partner, partner_sems.at[0], partner_sems.at[1], partner)
    first.start()
    first.wait()
    pair[...] = g_ref[:, :, h] + from_partner[...]
    down = send(pair.at[:, 1], from_prev, chain_sems.at[0], chain_sems.at[1], after)
    up = send(pair.at[:, 0], from_next, chain_sems.at[2], chain_sems.at[3], before)

    @pl.when(has_next)
    def _():
        down.start()

    @pl.when(has_prev)
    def _():
        up.start()

    @pl.when(has_prev)
    def _():
        down.wait_recv()
        own[:, 0] = pair[:, 0] + from_prev[...]

    @pl.when(jnp.logical_not(has_prev))
    def _():
        own[:, 0] = pair[:, 0]

    top = own[:, 0]
    squares = jnp.sum(top * top, axis=0)
    squares = jnp.sum(squares.reshape(-1, 8, width), axis=0)
    folded = squares[:, :128]
    for lane in range(128, width, 128):
        folded = folded + squares[:, lane : lane + 128]
    tile[...] = folded
    sends_a = [
        send(tile, tiles_a.at[d - 1], a_send.at[d - 1], a_recv.at[d - 1], (s, (m + d) % group))
        for d in range(1, group)
    ]
    for copy in sends_a:
        copy.start()

    @pl.when(has_next)
    def _():
        up.wait_recv()
        own[:, 1] = pair[:, 1] + from_next[...]

    @pl.when(jnp.logical_not(has_next))
    def _():
        own[:, 1] = jnp.zeros_like(from_next)

    second = send(own, other, back_sems.at[0], back_sems.at[1], partner)
    second.start()

    total = tile[...]
    for d in range(1, group):
        sends_a[d - 1].wait_recv()
        total = total + tiles_a[d - 1]
    sum_a[...] = total
    sends_b = [
        send(sum_a, tiles_b.at[d - 1], b_send.at[d - 1], b_recv.at[d - 1], ((s + d) % strips, m))
        for d in range(1, strips)
    ]
    for copy in sends_b:
        copy.start()
    second.wait_recv()
    for d in range(1, strips):
        sends_b[d - 1].wait_recv()
        total = total + tiles_b[d - 1]
    total = jnp.sum(jnp.sum(total, axis=1, keepdims=True), axis=0, keepdims=True)
    factor = step_scale / jnp.sqrt(total / (cells * copies) + epsilon)
    factor = factor.reshape(1, 1, 1, 1)
    out_ref[:, :, h] = rows_ref[:, :, h] + factor * own[...]
    out_ref[:, :, 1 - h] = rows_ref[:, :, 1 - h] + factor * other[...]

    @pl.when(has_next)
    def _():
        down.wait_send()

    @pl.when(has_prev)
    def _():
        up.wait_send()

    for copy in sends_a + [second] + sends_b:
        copy.wait_send()


def exchange(grad, rows, copies, slots, cells):
    strips, group = lax.axis_size("strip"), lax.axis_size("mode")
    parts, total_rows, width = rows.shape
    quarter = total_rows // 4
    shape = (parts, 2, 2, quarter, width)
    vmem = pl.BlockSpec(memory_space=pltpu.VMEM)
    mine = pltpu.VMEM((parts, 2, quarter, width), f32)
    piece = pltpu.VMEM((parts, quarter, width), f32)
    dma = pltpu.SemaphoreType.DMA
    out = pl.pallas_call(
        functools.partial(exchange_kernel, copies, slots, float(cells)),
        out_shape=jax.ShapeDtypeStruct(shape, f32),
        in_specs=[vmem, vmem],
        out_specs=vmem,
        scratch_shapes=[
            mine, mine, piece, piece, mine, mine,
            pltpu.VMEM((8, 128), f32),
            pltpu.VMEM((group - 1, 8, 128), f32),
            pltpu.VMEM((8, 128), f32),
            pltpu.VMEM((strips - 1, 8, 128), f32),
            dma((2,)), dma((4,)), dma((2,)),
            dma((group - 1,)), dma((group - 1,)), dma((strips - 1,)), dma((strips - 1,)),
        ],
        compiler_params=pltpu.CompilerParams(collective_id=0, has_side_effects=True, vmem_limit_bytes=32 * 2**20),
        name="exchange",
    )(grad.reshape(shape), rows.reshape(shape))
    return out.reshape(rows.shape)


def body(object_field, probe_modes, measured, positions):
    strips, group = lax.axis_size("strip"), lax.axis_size("mode")
    stripe_rows, width = object_field.shape[1:]
    n = probe_modes.shape[2]
    local = probe_modes.shape[1]
    slots = positions.shape[1]
    copies = group // slots
    halo = HALO
    s, m = lax.axis_index("strip"), lax.axis_index("mode")
    side = s % 2
    q = m // copies
    mine = (q // 2) == side
    consts = tables(n)
    partner = [(i, i ^ 1) for i in range(strips)]

    def window_of(which):
        upper = jnp.where(which == 0, 2, 1)
        lower = jnp.where(which == 0, 0, 3)
        return jnp.where(q % 2 == 0, upper, lower)

    share = n // strips
    piece = lax.dynamic_slice_in_dim(probe_modes, s * share, share, axis=2)
    pieces = lax.all_gather(piece, ("strip", "mode"))
    pieces = pieces.reshape(strips, group, 2, local, share, n)
    probe = pieces.transpose(2, 1, 3, 0, 4, 5).reshape(2, group * local, n, n)

    below = lax.ppermute(object_field[:, :halo], "strip", [(i + 1, i) for i in range(strips - 1)])
    frame = jnp.concatenate([object_field, below], axis=1)
    own_rows = jnp.where(q % 2 == 0, frame[:, :stripe_rows], frame[:, halo:])
    theirs = lax.ppermute(own_rows, "strip", partner)
    rows = jnp.where(mine, own_rows, theirs)

    pick = lambda which: lax.dynamic_index_in_dim(measured[0], window_of(which), 0, keepdims=False)
    meas = jnp.where(mine, pick(side), lax.ppermute(pick(1 - side), "strip", partner))
    meas = meas.reshape(n // 2, 2, n // 2, 2).transpose(1, 0, 3, 2).reshape(n, n)
    at = lambda which: lax.dynamic_index_in_dim(positions[0, :, 1], window_of(which), 0)
    col = jnp.where(mine, at(side), lax.ppermute(at(1 - side), "strip", partner))

    cells = stripe_rows * strips * width
    for iteration in range(ITERS):
        grad = window_gradient(col, rows, probe, meas, consts)
        rows = exchange(grad, rows, copies, slots, cells)

    part_rows = halo // 2
    mine_part = lax.dynamic_slice_in_dim(rows, side * part_rows, part_rows, axis=1)
    parts = lax.all_gather(mine_part, "mode")[::copies]
    keep = lax.dynamic_slice_in_dim(parts, 2 * side, 2, axis=0)
    give = lax.dynamic_slice_in_dim(parts, 2 * (1 - side), 2, axis=0)
    got = lax.ppermute(give, "strip", partner)
    low = jnp.where(side == 0, keep, got)
    high = jnp.where(side == 0, got, keep)
    whole = jnp.concatenate([low, high], axis=2)
    return whole.transpose(1, 0, 2, 3).reshape(2, stripe_rows, width)


def solution(mesh):
    return jax.shard_map(
        body,
        mesh=mesh,
        in_specs=(
            P(None, "strip", None),
            P(None, "mode", None, None),
            P("strip", None, None, None),
            P("strip", None, None),
        ),
        out_specs=P(None, "strip", None),
        check_vma=False,
    )
```

```python
import functools

import jax
import jax.numpy as jnp
import numpy as np
from jax import lax
from jax.experimental import pallas as pl
from jax.experimental.pallas import tpu as pltpu
from jax.sharding import PartitionSpec as P

HALO = 128
ITERS = 3

regularizer = 0.1
step_scale = 0.3
epsilon = 1e-06
f32 = jnp.float32
bf16 = jnp.bfloat16
MESH = pl.DeviceIdType.MESH


def tables(n):
    half = n // 2
    k = np.arange(half)
    angle = 2.0 * np.pi * (np.outer(k, k) % half) / half
    c = np.cos(angle) / np.sqrt(n)
    s = np.sin(angle) / np.sqrt(n)
    right_f = np.block([[c, -s], [s, c]])
    right_i = np.block([[c, s], [-s, c]])
    turn = 2.0 * np.pi * k / n
    wr, wi = np.cos(turn), -np.sin(turn)

    def split(t):
        t = jnp.asarray(t, f32)
        high = t.astype(bf16)
        low = (t - high.astype(f32)).astype(bf16)
        return high, low

    rf, ri = split(right_f), split(right_i)
    lf, li = split(right_f.T), split(right_i.T)
    rights = jnp.stack([rf[0], rf[1], ri[0], ri[1]])
    lefts = jnp.stack([jnp.concatenate(lf), jnp.concatenate(li)])
    lanes = jnp.asarray(np.stack([wr, wi]), f32)[:, None, :]
    subs = jnp.asarray(np.broadcast_to(np.stack([wr, wi])[:, :, None], (2, half, n)), f32)
    return rights, lefts, lanes, subs


def split2(x):
    high = x.astype(bf16)
    low = (x - high.astype(f32)).astype(bf16)
    return high, low


def dot(a, b):
    return jnp.dot(a, b, preferred_element_type=f32)


def right_dot(x, t_high, t_low):
    high, low = split2(x)
    return dot(high, t_high) + (dot(low, t_high) + dot(high, t_low))


def left_dot(t_both, x):
    n = x.shape[0]
    high, low = split2(x)
    both = dot(t_both, high)
    return both[:n] + (both[n:] + dot(t_both[:n], low))


def gradient_kernel(col_ref, obj_ref, kept_ref, came_ref, meas_ref, rights, lefts, lanes, subs, out_ref, far_ref, power_ref, acc_ref, patch_ref):
    n = meas_ref.shape[0]
    half = n // 2
    width = obj_ref.shape[2]
    modes = kept_ref.shape[0]
    col, side = col_ref[0], col_ref[1]
    back = jnp.where(col == 0, 0, width - col)
    for part in range(2):
        patch_ref[part] = pltpu.roll(obj_ref[part], back, 1)[:, :n]
    power_ref[...] = jnp.zeros_like(power_ref)
    acc_ref[...] = jnp.zeros_like(acc_ref)
    cat = jnp.concatenate

    def probe_of(m):
        kept, came = kept_ref[m], came_ref[m]
        return jnp.where(side == 0, kept, came), jnp.where(side == 0, came, kept)

    def forward(m):
        pr, pi = probe_of(m)
        xr, xi = patch_ref[0], patch_ref[1]
        er = pr * xr - pi * xi
        ei = pr * xi + pi * xr
        wr, wi = lanes[0], lanes[1]
        ar, ai = er[:, :half] + er[:, half:], ei[:, :half] + ei[:, half:]
        br, bi = er[:, :half] - er[:, half:], ei[:, :half] - ei[:, half:]
        even = right_dot(cat([ar, ai], 1), rights[0], rights[1])
        odd = right_dot(cat([br * wr - bi * wi, br * wi + bi * wr], 1), rights[0], rights[1])
        yr = cat([even[:, :half], odd[:, :half]], 1)
        yi = cat([even[:, half:], odd[:, half:]], 1)
        wr, wi = subs[0], subs[1]
        ar, ai = yr[:half] + yr[half:], yi[:half] + yi[half:]
        br, bi = yr[:half] - yr[half:], yi[:half] - yi[half:]
        even = left_dot(lefts[0], cat([ar, ai], 0))
        odd = left_dot(lefts[0], cat([br * wr - bi * wi, br * wi + bi * wr], 0))
        far_ref[m, 0] = even
        far_ref[m, 1] = odd
        return cat(
            [
                even[:half] * even[:half] + even[half:] * even[half:],
                odd[:half] * odd[:half] + odd[half:] * odd[half:],
            ],
            0,
        )

    def forward_two(i, carry):
        power_ref[...] += forward(2 * i) + forward(2 * i + 1)
        return carry

    lax.fori_loop(0, modes // 2, forward_two, 0)
    power_ref[...] = jnp.sqrt((meas_ref[...] + regularizer) / (power_ref[...] + regularizer)) - 1.0

    def backward(m):
        ce, co = power_ref[:half], power_ref[half:]
        ce, co = cat([ce, ce], 0), cat([co, co], 0)
        even = left_dot(lefts[1], ce * far_ref[m, 0])
        odd = left_dot(lefts[1], co * far_ref[m, 1])
        wr, wi = subs[0], subs[1]
        ar, ai = even[:half], even[half:]
        br, bi = odd[:half], odd[half:]
        tr, ti = br * wr + bi * wi, bi * wr - br * wi
        yr = cat([ar + tr, ar - tr], 0)
        yi = cat([ai + ti, ai - ti], 0)
        even = right_dot(cat([yr[:, :half], yi[:, :half]], 1), rights[2], rights[3])
        odd = right_dot(cat([yr[:, half:], yi[:, half:]], 1), rights[2], rights[3])
        wr, wi = lanes[0], lanes[1]
        ar, ai = even[:, :half], even[:, half:]
        br, bi = odd[:, :half], odd[:, half:]
        tr, ti = br * wr + bi * wi, bi * wr - br * wi
        dr = cat([ar + tr, ar - tr], 1)
        di = cat([ai + ti, ai - ti], 1)
        pr, pi = probe_of(m)
        return pr * dr + pi * di, pr * di - pi * dr

    def backward_two(i, carry):
        gr, gi = backward(2 * i)
        hr, hi = backward(2 * i + 1)
        acc_ref[0] += gr + hr
        acc_ref[1] += gi + hi
        return carry

    lax.fori_loop(0, modes // 2, backward_two, 0)
    for part in range(2):
        wide = cat([acc_ref[part], jnp.zeros((n, width - n), f32)], 1)
        out_ref[part] = pltpu.roll(wide, col, 1)


def window_gradient(col, rows, probe, meas, consts):
    n = meas.shape[0]
    modes = probe[0].shape[0]
    vmem = pl.BlockSpec(memory_space=pltpu.VMEM)
    flops = modes * 2 * 4 * 3 * 2 * n**3
    return pl.pallas_call(
        gradient_kernel,
        out_shape=jax.ShapeDtypeStruct(rows.shape, f32),
        in_specs=[pl.BlockSpec(memory_space=pltpu.SMEM)] + [vmem] * 8,
        out_specs=vmem,
        scratch_shapes=[
            pltpu.VMEM((modes, 2, n, n), f32),
            pltpu.VMEM((n, n), f32),
            pltpu.VMEM((2, n, n), f32),
            pltpu.VMEM((2, n, n), f32),
        ],
        cost_estimate=pl.CostEstimate(flops=flops, bytes_accessed=8 * modes * n * n, transcendentals=n * n),
        compiler_params=pltpu.CompilerParams(vmem_limit_bytes=48 * 2**20),
        name="window_gradient",
    )(col, rows, *probe, meas, *consts)


def exchange_kernel(copies, slots, cells, g_ref, rows_ref, out_ref, pair, from_partner, from_prev, from_next, own, other, tile, tiles_a, sum_a, tiles_b, partner_sems, chain_sems, back_sems, a_send, a_recv, b_send, b_recv):
    strips, group = lax.axis_size("strip"), lax.axis_size("mode")
    s, m = lax.axis_index("strip"), lax.axis_index("mode")
    h, q = s % 2, m // copies
    width = g_ref.shape[-1]
    partner = (s + 1 - 2 * h, m)
    inner_next, inner_prev = q < slots - 1, q > 0
    has_next = jnp.logical_or(inner_next, s < strips - 2)
    has_prev = jnp.logical_or(inner_prev, s >= 2)
    cross = (slots - 1) * copies
    after = (jnp.where(inner_next, s, s + 2), jnp.where(inner_next, m + copies, m - cross))
    before = (jnp.where(inner_prev, s, s - 2), jnp.where(inner_prev, m - copies, m + cross))
    cross_next = jnp.logical_and(has_next, jnp.logical_not(inner_next))
    cross_prev = jnp.logical_and(has_prev, jnp.logical_not(inner_prev))

    barrier = pltpu.get_barrier_semaphore()

    def greet(device):
        pl.semaphore_signal(barrier, inc=1, device_id=device, device_id_type=MESH)

    for d in range(1, group):
        greet((s, (m + d) % group))
    for d in range(1, strips):
        greet(((s + d) % strips, m))

    @pl.when(cross_next)
    def _():
        greet(after)

    @pl.when(cross_prev)
    def _():
        greet(before)

    extra = jnp.where(cross_next, 1, 0) + jnp.where(cross_prev, 1, 0)
    pl.semaphore_wait(barrier, group + strips - 2 + extra)

    def send(src, dst, send_sem, recv_sem, device):
        return pltpu.make_async_remote_copy(
            src_ref=src, dst_ref=dst, send_sem=send_sem, recv_sem=recv_sem,
            device_id=device, device_id_type=MESH,
        )

    first = send(g_ref.at[:, :, 1 - h], from_partner, partner_sems.at[0], partner_sems.at[1], partner)
    first.start()
    first.wait()
    pair[...] = g_ref[:, :, h] + from_partner[...]
    down = send(pair.at[:, 1], from_prev, chain_sems.at[0], chain_sems.at[1], after)
    up = send(pair.at[:, 0], from_next, chain_sems.at[2], chain_sems.at[3], before)

    @pl.when(has_next)
    def _():
        down.start()

    @pl.when(has_prev)
    def _():
        up.start()

    @pl.when(has_prev)
    def _():
        down.wait_recv()
        own[:, 0] = pair[:, 0] + from_prev[...]

    @pl.when(jnp.logical_not(has_prev))
    def _():
        own[:, 0] = pair[:, 0]

    top = own[:, 0]
    squares = jnp.sum(top * top, axis=0)
    squares = jnp.sum(squares.reshape(-1, 8, width), axis=0)
    folded = squares[:, :128]
    for lane in range(128, width, 128):
        folded = folded + squares[:, lane : lane + 128]
    tile[...] = folded
    sends_a = [
        send(tile, tiles_a.at[d - 1], a_send.at[d - 1], a_recv.at[d - 1], (s, (m + d) % group))
        for d in range(1, group)
    ]
    for copy in sends_a:
        copy.start()

    @pl.when(has_next)
    def _():
        up.wait_recv()
        own[:, 1] = pair[:, 1] + from_next[...]

    @pl.when(jnp.logical_not(has_next))
    def _():
        own[:, 1] = jnp.zeros_like(from_next)

    second = send(own, other, back_sems.at[0], back_sems.at[1], partner)
    second.start()

    total = tile[...]
    for d in range(1, group):
        sends_a[d - 1].wait_recv()
        total = total + tiles_a[d - 1]
    sum_a[...] = total
    sends_b = [
        send(sum_a, tiles_b.at[d - 1], b_send.at[d - 1], b_recv.at[d - 1], ((s + d) % strips, m))
        for d in range(1, strips)
    ]
    for copy in sends_b:
        copy.start()
    second.wait_recv()
    for d in range(1, strips):
        sends_b[d - 1].wait_recv()
        total = total + tiles_b[d - 1]
    total = jnp.sum(jnp.sum(total, axis=1, keepdims=True), axis=0, keepdims=True)
    factor = step_scale / jnp.sqrt(total / (cells * copies) + epsilon)
    factor = factor.reshape(1, 1, 1, 1)
    out_ref[:, :, h] = rows_ref[:, :, h] + factor * own[...]
    out_ref[:, :, 1 - h] = rows_ref[:, :, 1 - h] + factor * other[...]

    @pl.when(has_next)
    def _():
        down.wait_send()

    @pl.when(has_prev)
    def _():
        up.wait_send()

    for copy in sends_a + [second] + sends_b:
        copy.wait_send()


def exchange(grad, rows, copies, slots, cells):
    strips, group = lax.axis_size("strip"), lax.axis_size("mode")
    parts, total_rows, width = rows.shape
    quarter = total_rows // 4
    shape = (parts, 2, 2, quarter, width)
    vmem = pl.BlockSpec(memory_space=pltpu.VMEM)
    mine = pltpu.VMEM((parts, 2, quarter, width), f32)
    piece = pltpu.VMEM((parts, quarter, width), f32)
    dma = pltpu.SemaphoreType.DMA
    out = pl.pallas_call(
        functools.partial(exchange_kernel, copies, slots, float(cells)),
        out_shape=jax.ShapeDtypeStruct(shape, f32),
        in_specs=[vmem, vmem],
        out_specs=vmem,
        scratch_shapes=[
            mine, mine, piece, piece, mine, mine,
            pltpu.VMEM((8, 128), f32),
            pltpu.VMEM((group - 1, 8, 128), f32),
            pltpu.VMEM((8, 128), f32),
            pltpu.VMEM((strips - 1, 8, 128), f32),
            dma((2,)), dma((4,)), dma((2,)),
            dma((group - 1,)), dma((group - 1,)), dma((strips - 1,)), dma((strips - 1,)),
        ],
        compiler_params=pltpu.CompilerParams(collective_id=0, has_side_effects=True, vmem_limit_bytes=32 * 2**20),
        name="exchange",
    )(grad.reshape(shape), rows.reshape(shape))
    return out.reshape(rows.shape)


def body(object_field, probe_modes, measured, positions):
    strips, group = lax.axis_size("strip"), lax.axis_size("mode")
    stripe_rows, width = object_field.shape[1:]
    n = probe_modes.shape[2]
    local = probe_modes.shape[1]
    slots = positions.shape[1]
    copies = group // slots
    halo = HALO
    s, m = lax.axis_index("strip"), lax.axis_index("mode")
    side = s % 2
    q = m // copies
    mine = (q // 2) == side
    consts = tables(n)
    partner = [(i, i ^ 1) for i in range(strips)]

    def window_of(which):
        upper = jnp.where(which == 0, 2, 1)
        lower = jnp.where(which == 0, 0, 3)
        return jnp.where(q % 2 == 0, upper, lower)

    half_probe = lax.dynamic_index_in_dim(probe_modes, side, 0, keepdims=False)
    kept = lax.all_gather(half_probe, "mode", tiled=True)
    below = lax.ppermute(object_field[:, :halo], "strip", [(i + 1, i) for i in range(strips - 1)])
    frame = jnp.concatenate([object_field, below], axis=1)
    own_rows = jnp.where(q % 2 == 0, frame[:, :stripe_rows], frame[:, halo:])
    theirs = lax.ppermute(own_rows, "strip", partner)
    rows = jnp.where(mine, own_rows, theirs)

    pick = lambda which: lax.dynamic_index_in_dim(measured[0], window_of(which), 0, keepdims=False)
    meas = jnp.where(mine, pick(side), lax.ppermute(pick(1 - side), "strip", partner))
    order = np.concatenate([np.arange(0, n, 2), np.arange(1, n, 2)])
    place = jnp.asarray(np.eye(n)[order], f32)
    exact = functools.partial(jnp.dot, precision=lax.Precision.HIGHEST)
    meas = exact(exact(place, meas), place.T)
    at = lambda which: lax.dynamic_index_in_dim(positions[0, :, 1], window_of(which), 0)
    col = jnp.where(mine, at(side), lax.ppermute(at(1 - side), "strip", partner))
    col = jnp.concatenate([col, side.reshape(1).astype(col.dtype)])
    kept, meas, rows, col = lax.optimization_barrier((kept, meas, rows, col))
    probe = (kept, lax.ppermute(kept, "strip", partner))

    cells = stripe_rows * strips * width
    for iteration in range(ITERS):
        grad = window_gradient(col, rows, probe, meas, consts)
        rows = exchange(grad, rows, copies, slots, cells)

    part_rows = halo // 2
    mine_part = lax.dynamic_slice_in_dim(rows, side * part_rows, part_rows, axis=1)
    parts = lax.all_gather(mine_part, "mode")[::copies]
    keep = lax.dynamic_slice_in_dim(parts, 2 * side, 2, axis=0)
    give = lax.dynamic_slice_in_dim(parts, 2 * (1 - side), 2, axis=0)
    got = lax.ppermute(give, "strip", partner)
    low = jnp.where(side == 0, keep, got)
    high = jnp.where(side == 0, got, keep)
    whole = jnp.concatenate([low, high], axis=2)
    return whole.transpose(1, 0, 2, 3).reshape(2, stripe_rows, width)


def solution(mesh):
    return jax.shard_map(
        body,
        mesh=mesh,
        in_specs=(
            P(None, "strip", None),
            P(None, "mode", None, None),
            P("strip", None, None, None),
            P("strip", None, None),
        ),
        out_specs=P(None, "strip", None),
        check_vma=False,
    )
```
